32 devices in a mesh: dp: 4 (over y, core), expert: 4 (over z), shard: 2 (over x).
Axes of the slice: x: 2, y: 2, z: 4, core: 2. Of those that a mesh axis runs over, the one named last changes fastest.
Arguments:
- tokens: bfloat16 [4096, 2048], P(('dp', 'expert'), 'shard'), may hold values from -6 to 6
- out_grad: bfloat16 [4096, 2048], P(('dp', 'expert'), 'shard'), may hold values from -6 to 6
- expert_ids: int32 [4096, 1], P(('dp', 'expert')), may hold values from 0 to 3; in each aligned block of 256 rows (0 to 255, 256 to 511, ...) at most 128 rows name the same one
- combine: float32 [4096, 1], P(('dp', 'expert')), may hold values from 0.05 to 0.45
- old_place: int32 [4], replicated, may hold values from 0 to 3, as said below
- new_place: int32 [4], replicated, may hold values from 0 to 3
- master: float32 [4, 3, 384, 2048], P('expert', None, 'shard', 'dp'), may hold values from -0.125 to 0.125
- moment_one: float32 [4, 3, 384, 2048], P('expert', None, 'shard', 'dp'), may hold values from -4 to 4
- moment_two: float32 [4, 3, 384, 2048], P('expert', None, 'shard', 'dp'), may hold values from 0.5 to 8
Outputs:
- token_grad: bfloat16 [4096, 2048], P(('dp', 'expert'), 'shard')
- master_out: float32 [4, 3, 384, 2048], P('expert', None, 'shard', 'dp')
- first_out: float32 [4, 3, 384, 2048], P('expert', None, 'shard', 'dp')
- second_out: float32 [4, 3, 384, 2048], P('expert', None, 'shard', 'dp')
The draws below stay inside these ranges and needn't reach their ends.
Inputs may be any that keep to these rules, and one draw needn't show every extreme that they name: old_place is a permutation of the owners; new_place equals old_place except in exactly 4 entries, which hold a cyclic rotation of those entries' owners. `expert_ids`: each token names exactly one expert of the window; among the 256 rows of one block no expert is named more than 128 times, a bound that some block reaches.
All inputs are finite; a program needn't handle non-finite values.
Results may differ from the reference program's by a relative error of at most 0.012.
Values may be sent and summed in bfloat16 or wider, within the bound.
No kernel may reach another device: no remote copies, remote signals or barrier semaphores. Data moves between devices by JAX's collectives and lax.ppermute only.
A program may use at most 64 MiB of HBM per device.

```python
import math
import jax
import jax.numpy as jnp
import numpy as np
from jax import lax

D = 2048
FF = 384
TOPW = 1
TOK_DEV = 256
EXPERTS = 4
HOT = 4
CAP = 128
TOKENS = 4096
N_DP = 4
N_EXPERT = 4
N_SHARD = 2


def placement_pair(key):
    mixed = jax.random.fold_in(key, 4242)
    key_one, key_two = jax.random.split(mixed)
    before = jax.random.permutation(key_one, EXPERTS).astype(jnp.int32)
    shuffled = jax.random.permutation(key_two, EXPERTS).astype(jnp.int32)
    moving = shuffled[:HOT]
    rotated = jnp.roll(moving, -1)
    after = before.at[moving].set(before[rotated])
    return (before, after)


def draw_old_place(key, part):
    return placement_pair(key)[0]


def draw_new_place(key, part):
    return placement_pair(key)[1]


def level_of(stream_key, shape, pieces, smallest, top_value):
    gain = 1.0
    for dim, parts in pieces:
        steps = jax.random.uniform(jax.random.fold_in(jax.random.fold_in(stream_key, 6), dim), (parts,), jnp.float32, smallest / len(pieces), top_value / len(pieces))
        gain = gain * jnp.repeat(jnp.exp(steps), shape[dim] // parts).reshape((-1,) + (1,) * (len(shape) - 1 - dim))
    return gain


def assign_block(stream_key, own, number, rows, number_of, top, most, slope):
    sequence = jax.random.permutation(stream_key, number_of)
    crowded, usual = shares(number_of, rows * top, most, slope, True), shares(number_of, rows * top, most, slope, False)
    places = jnp.arange(number_of)

    def named(lengths, offset_by):
        used = int((lengths > 0).sum())
        fixed = max(1, used // 4)
        passed = fixed + (places - fixed + offset_by * (used - fixed)) % max(1, number_of - fixed)
        return jnp.zeros((number_of,), jnp.int32).at[sequence[jnp.where(places < fixed, places, passed)]].set(jnp.asarray(lengths, jnp.int32))

    lengths = jnp.where(number % 4 == 0, named(crowded, number // 4), named(usual, number - number // 4 - 1))
    mixed = jax.random.permutation(jax.random.fold_in(own, 3), number_of)
    donor, receiver = mixed[0:number_of // 2 * 2:2], mixed[1:number_of // 2 * 2:2]
    margin = jnp.minimum(lengths[donor] - 1, most - lengths[receiver]) // 2
    margin = jnp.where((donor == sequence[0]) | (receiver == sequence[0]) | (lengths[receiver] == 0), 0, jnp.maximum(margin, 0))
    passed = jax.random.randint(jax.random.fold_in(own, 4), (number_of // 2,), 0, 1 << 20) % (margin + 1)
    lengths = lengths.at[donor].add(-passed).at[receiver].add(passed)
    items = jnp.searchsorted(jnp.cumsum(lengths), jnp.arange(rows * top), side="right").astype(jnp.int32)
    table = items.reshape(top, rows).T
    table = table[jax.random.permutation(jax.random.fold_in(own, 1), rows)]
    offset_by = jax.random.randint(jax.random.fold_in(own, 2), (rows, 1), 0, top)
    return jnp.take_along_axis(table, (jnp.arange(top)[None, :] + offset_by) % top, axis=1)


def shares(number_of, total, most, slope, full):
    loads = [(1 << 20) // math.isqrt(rank ** slope) + 1 for rank in range(1, number_of + 1)]
    largest = most if full else min(most, max(-(-total // number_of), total * loads[0] // sum(loads)))
    least = 1 if total - largest >= number_of - 1 else 0
    holding, rest = [largest] + [least] * (number_of - 1), total - largest - least * (number_of - 1)
    while rest > 0:
        free = [i for i in range(1, number_of) if holding[i] < largest] or [i for i in range(1, number_of) if holding[i] < most]
        pool, left = sum([loads[i] for i in free]), rest
        for i in free:
            extra = min(most - holding[i], max(1, left * loads[i] // pool), rest)
            holding[i] = holding[i] + extra
            rest = rest - extra
    return np.array(holding)


def noise(stream_key, dims, deviation, bound, cuts=(), kind=jnp.bfloat16):
    drawn = deviation * jax.random.normal(stream_key, dims, jnp.float32)
    if cuts:
        drawn = drawn * level_of(stream_key, dims, cuts, -0.22, 0.18)
    return jnp.clip(drawn, -bound, bound).astype(kind)


def setup_inputs(seed: int = 0) -> dict:
    streams_of = jax.random.split(jax.random.key(seed), 10)
    tokens = noise(streams_of[0], (TOKENS, D), 1.0, 6.0, ((0, 16), (1, 2)))
    out_grad = noise(streams_of[1], (TOKENS, D), 1.0, 6.0, ((0, 16), (1, 2)))
    expert_ids_keys = jax.random.split(jax.random.fold_in(streams_of[2], 1), TOKENS // TOK_DEV)
    expert_ids_turns = jax.random.permutation(jax.random.fold_in(streams_of[2], 3), TOKENS // TOK_DEV)
    expert_ids = jax.vmap(lambda own, number: assign_block(jax.random.fold_in(streams_of[2], 2), own, number, TOK_DEV, EXPERTS, TOPW, CAP, 2))(expert_ids_keys, expert_ids_turns).reshape((TOKENS, TOPW))
    combine = jnp.clip(0.05 + 0.39999999 * jax.random.uniform(streams_of[3], (TOKENS, TOPW), jnp.float32) ** level_of(streams_of[3], (TOKENS, TOPW), ((0, 16),), -0.2, 0.2), 0.05, 0.45)
    old_place = draw_old_place(jax.random.fold_in(streams_of[9], 71), 0)
    new_place = draw_new_place(jax.random.fold_in(streams_of[9], 71), 0)
    master = noise(streams_of[6], (EXPERTS, 3, FF, D), D ** -0.5, 0.125, ((0, 4), (2, 2), (3, 4)), jnp.float32)
    moment_one = noise(streams_of[7], (EXPERTS, 3, FF, D), 0.5, 4.0, ((0, 4), (2, 2), (3, 4)), jnp.float32)
    moment_two = jnp.clip(jnp.exp(math.log(8.0) - 2.7725887 * jax.random.uniform(streams_of[8], (EXPERTS, 3, FF, D), jnp.float32) ** level_of(streams_of[8], (EXPERTS, 3, FF, D), ((0, 4), (2, 2), (3, 4)), -0.2, 0.2)), 0.5, 8.0)
    return dict(tokens=tokens, out_grad=out_grad, expert_ids=expert_ids, combine=combine, old_place=old_place, new_place=new_place, master=master, moment_one=moment_one, moment_two=moment_two)


beta_first = 0.9
beta_second = 0.95
adam_epsilon = 1e-08
learn_rate = 0.001
weight_decay = 0.1
bias_first = 1.0 - beta_first ** 10
bias_second = 1.0 - beta_second ** 10

def adamw_step(master, moment_one, moment_two, gradient):
    first_out = beta_first * moment_one + (1.0 - beta_first) * gradient
    second_out = beta_second * moment_two + (1.0 - beta_second) * gradient * gradient
    update = first_out / bias_first / (jnp.sqrt(second_out / bias_second) + adam_epsilon)
    master_out = master - learn_rate * (update + weight_decay * master)
    return (master_out, first_out, second_out)

def reference(tokens, out_grad, expert_ids, combine, old_place, new_place, master, moment_one, moment_two):
    owners = jnp.arange(EXPERTS, dtype=jnp.int32)
    holds = (new_place[:, None] == owners[None, :]).astype(jnp.int32)
    source_owner = lax.optimization_barrier(jnp.sum(old_place[:, None] * holds, axis=0)).astype(jnp.int32)
    moved_master = master[source_owner]
    moved_one = moment_one[source_owner]
    moved_two = moment_two[source_owner]
    weights = moved_master.astype(jnp.bfloat16)
    blocks = N_DP * N_EXPERT
    assign = TOK_DEV * TOPW
    flat_ids = expert_ids.reshape(blocks, assign)
    onehot = (flat_ids[:, :, None] == owners[None, None, :]).astype(jnp.int32)
    earlier = jnp.cumsum(onehot, axis=1) - onehot
    slot = lax.optimization_barrier(jnp.sum(earlier * onehot, axis=2)).astype(jnp.int32)
    target = lax.optimization_barrier(jnp.sum(onehot * new_place[None, None, :], axis=2)).astype(jnp.int32)
    block_index = jnp.arange(blocks, dtype=jnp.int32)[:, None]
    replica = block_index // N_EXPERT
    sender = block_index % N_EXPERT
    position = ((target * N_DP + replica) * N_EXPERT + sender) * CAP + slot
    token_index = block_index * TOK_DEV + jnp.arange(assign, dtype=jnp.int32)[None, :] // TOPW
    row_count = N_DP * N_EXPERT * CAP
    table = jnp.zeros((EXPERTS * row_count,), jnp.int32).at[position.reshape(-1)].set(token_index.reshape(-1) + 1)
    scales = jnp.zeros((EXPERTS * row_count,), jnp.float32).at[position.reshape(-1)].set(combine.reshape(-1))
    table = table.reshape(EXPERTS, row_count)
    scales = scales.reshape(EXPERTS, row_count)
    width_f = FF // N_SHARD

    def per_owner(inputs):
        row_table, row_scale, weight, master_own, first_own, second_own = inputs
        valid = row_table > 0
        picked = jnp.maximum(row_table - 1, 0)
        rows_x = jnp.where(valid[:, None], tokens[picked], jnp.zeros((), jnp.bfloat16)).astype(jnp.bfloat16)
        rows_dy = jnp.where(valid[:, None], row_scale[:, None] * out_grad[picked].astype(jnp.float32), jnp.zeros((), jnp.float32)).astype(jnp.bfloat16)
        gate_pre = jnp.dot(rows_x, weight[0].T, preferred_element_type=jnp.float32)
        up_pre = jnp.dot(rows_x, weight[1].T, preferred_element_type=jnp.float32)
        sigma = jax.nn.sigmoid(gate_pre)
        active = gate_pre * sigma
        hidden = (active * up_pre).astype(jnp.bfloat16)
        grad_hidden = jnp.dot(rows_dy, weight[2].T, preferred_element_type=jnp.float32)
        grad_up = (grad_hidden * active).astype(jnp.bfloat16)
        grad_gate = (grad_hidden * up_pre * sigma * (1.0 + gate_pre * (1.0 - sigma))).astype(jnp.bfloat16)
        gate_groups = grad_gate.reshape(row_count, N_SHARD, width_f).astype(jnp.float32)
        up_groups = grad_up.reshape(row_count, N_SHARD, width_f).astype(jnp.float32)
        gate_table = weight[0].reshape(N_SHARD, width_f, D).astype(jnp.float32)
        up_table = weight[1].reshape(N_SHARD, width_f, D).astype(jnp.float32)
        group_terms = jnp.einsum('rsf,sfd->srd', gate_groups, gate_table) + jnp.einsum('rsf,sfd->srd', up_groups, up_table)
        group_terms = lax.optimization_barrier(group_terms.astype(jnp.bfloat16))
        row_grad = lax.optimization_barrier(jnp.sum(group_terms.astype(jnp.float32), axis=0))
        x_rep = rows_x.reshape(N_DP, -1, D).astype(jnp.float32)
        dy_rep = rows_dy.reshape(N_DP, -1, D).astype(jnp.float32)
        gate_rep = grad_gate.reshape(N_DP, -1, FF).astype(jnp.float32)
        up_rep = grad_up.reshape(N_DP, -1, FF).astype(jnp.float32)
        hidden_rep = hidden.reshape(N_DP, -1, FF).astype(jnp.float32)
        replica_grad = jnp.stack([jnp.einsum('prf,prd->pfd', gate_rep, x_rep), jnp.einsum('prf,prd->pfd', up_rep, x_rep), jnp.einsum('prf,prd->pfd', hidden_rep, dy_rep)], axis=1)
        replica_grad = lax.optimization_barrier(replica_grad.astype(jnp.bfloat16))
        gradient = lax.optimization_barrier(jnp.sum(replica_grad.astype(jnp.float32), axis=0))
        master_new, first_new, second_new = adamw_step(master_own, first_own, second_own, gradient)
        return (row_grad, master_new, first_new, second_new)
    row_grads, master_out, first_out, second_out = lax.map(per_owner, (table, scales, weights, moved_master, moved_one, moved_two))
    where_to = jnp.where(table > 0, table - 1, TOKENS).astype(jnp.int32).reshape(-1)
    token_grad = jnp.zeros((TOKENS, D), jnp.float32).at[where_to].add(row_grads.reshape(-1, D), mode='drop')
    return (token_grad.astype(jnp.bfloat16), master_out, first_out, second_out)
```

```python
import jax
import jax.numpy as jnp
from jax import lax
from jax.sharding import PartitionSpec as P

beta_first = 0.9
beta_second = 0.95
adam_epsilon = 1e-08
learn_rate = 0.001
weight_decay = 0.1
bias_first = 1.0 - beta_first**10
bias_second = 1.0 - beta_second**10

half = jnp.bfloat16
wide = jnp.float32


def adamw_step(master, moment_one, moment_two, gradient):
    first_out = beta_first * moment_one + (1.0 - beta_first) * gradient
    second_out = beta_second * moment_two + (1.0 - beta_second) * gradient * gradient
    update = first_out / bias_first / (jnp.sqrt(second_out / bias_second) + adam_epsilon)
    master_out = master - learn_rate * (update + weight_decay * master)
    return (master_out, first_out, second_out)


class Axis:
    def __init__(self, name):
        self.name = name
        self.size = lax.axis_size(name)
        self.me = lax.axis_index(name)
        self.pairs = self.size in (1, 2, 4)

    def peer(self, k):
        return self.me ^ k if self.pairs else jnp.int32(k)

    def entry(self, device):
        return self.me ^ device if self.pairs else device

    def swap(self, value, k):
        return lax.ppermute(value, self.name, [(i, i ^ k) for i in range(self.size)])

    def gather(self, value, near_first=True):
        if not self.pairs:
            every = lax.all_gather(value, self.name, axis=0, tiled=False)
            return [every[k] for k in range(self.size)]
        if self.size == 1:
            return [value]
        if self.size == 2:
            return [value, self.swap(value, 1)]
        first, second = (1, 2) if near_first else (2, 1)
        have = jnp.stack([value, self.swap(value, first)])
        got = self.swap(have, second)
        out = [have[0], None, None, None]
        out[first], out[second], out[3] = have[1], got[0], got[1]
        return out

    def exchange(self, values):
        if not self.pairs:
            every = lax.all_to_all(
                jnp.stack(values), self.name, split_axis=0, concat_axis=0, tiled=True
            )
            return [every[k] for k in range(self.size)]
        return [values[0]] + [self.swap(values[k], k) for k in range(1, self.size)]

    def scatter_sum(self, values, near_first=True):
        if not self.pairs:
            return lax.psum_scatter(
                jnp.stack(values).astype(half), self.name, scatter_dimension=0, tiled=False
            ).astype(wide)
        if self.size == 1:
            return values[0]
        if self.size == 2:
            return values[0] + self.swap(values[1].astype(half), 1).astype(wide)
        first, second = (1, 2) if near_first else (2, 1)
        got = self.swap(jnp.stack([values[first], values[3]]).astype(half), first)
        mine = values[0] + got[0].astype(wide)
        other = values[second] + got[1].astype(wide)
        return mine + self.swap(other.astype(half), second).astype(wide)


def pick(values, index):
    return lax.dynamic_index_in_dim(jnp.stack(values), index, axis=0, keepdims=False)


def rows_dot(a, b):
    return lax.dot_general(a, b, (((1,), (1,)), ((), ())), preferred_element_type=wide)


def sum_dot(a, b):
    return lax.dot_general(a, b, (((0,), (0,)), ((), ())), preferred_element_type=wide)


def on_device(
    tokens, out_grad, expert_ids, combine, old_place, new_place, master, moment_one, moment_two
):
    owner, shard, replica = Axis("expert"), Axis("shard"), Axis("dp")
    rows, column = tokens.shape
    part = master.shape[3]
    hidden_part = master.shape[2]

    ids = jnp.concatenate(replica.gather(expert_ids.reshape(rows)), axis=0)
    named = ids[:, None] == jnp.arange(old_place.shape[0], dtype=jnp.int32)[None, :]
    old_owner = jnp.sum(jnp.where(named, old_place[None, :], 0), axis=1)[:, None]
    new_owner = jnp.sum(jnp.where(named, new_place[None, :], 0), axis=1)[:, None]

    weight = master[0].astype(half)
    weights_gu = owner.gather(weight[:2], near_first=False)
    weights_d = owner.gather(weight[2], near_first=True)

    def columns_of(value):
        whole = jnp.concatenate([v[None] for v in shard.gather(value)], axis=0)
        per = max(part // column, 1)
        pieces = []
        for k in range(replica.size):
            start = replica.peer(k) * part
            if column >= part:
                slab = lax.dynamic_index_in_dim(
                    whole, shard.entry(start // column), axis=0, keepdims=False
                )
                pieces.append(lax.dynamic_slice_in_dim(slab, start % column, part, axis=1))
            else:
                pieces.append(
                    jnp.concatenate(
                        [
                            lax.dynamic_index_in_dim(
                                whole, shard.entry(start // column + j), axis=0, keepdims=False
                            )
                            for j in range(per)
                        ],
                        axis=1,
                    )
                )
        return jnp.concatenate(replica.exchange(pieces), axis=0)

    rows_x = columns_of(tokens)
    rows_dy = columns_of((combine * out_grad.astype(wide)).astype(half))

    none = jnp.zeros((), half)
    by_old = [old_owner == owner.peer(k) for k in range(owner.size)]
    by_new = [new_owner == owner.peer(k) for k in range(owner.size)]
    gate_up = jnp.zeros((rows_x.shape[0], 2 * hidden_part), wide)
    grad_hid = jnp.zeros((rows_x.shape[0], hidden_part), wide)
    for k in range(owner.size):
        gate_up += rows_dot(
            jnp.where(by_old[k], rows_x, none), weights_gu[k].reshape(2 * hidden_part, part)
        )
        grad_hid += rows_dot(jnp.where(by_old[k], rows_dy, none), weights_d[k])
    products = jnp.concatenate([gate_up, grad_hid], axis=1)
    own = replica.scatter_sum(
        [products[k * rows : (k + 1) * rows] for k in range(replica.size)], near_first=True
    )
    gate_pre = own[:, :hidden_part]
    up_pre = own[:, hidden_part : 2 * hidden_part]
    grad_hidden = own[:, 2 * hidden_part :]
    sigma = jax.nn.sigmoid(gate_pre)
    active = gate_pre * sigma
    hidden = (active * up_pre).astype(half)
    grad_up = (grad_hidden * active).astype(half)
    grad_gate = (grad_hidden * up_pre * sigma * (1.0 + gate_pre * (1.0 - sigma))).astype(half)
    every = jnp.concatenate(
        replica.gather(
            jnp.concatenate([grad_gate, grad_up, hidden], axis=1), near_first=False
        ),
        axis=0,
    )

    grads = []
    for k in range(owner.size):
        chosen = jnp.where(by_new[k], every, none)
        grads.append(
            (
                sum_dot(chosen[:, : 2 * hidden_part], rows_x).reshape(2, hidden_part, part),
                sum_dot(chosen[:, 2 * hidden_part :], rows_dy),
            )
        )
    gradient_gu = owner.scatter_sum([g[0] for g in grads], near_first=True)
    gradient_d = owner.scatter_sum([g[1] for g in grads], near_first=False)

    back = jnp.zeros((rows_x.shape[0], part), wide)
    for k in range(owner.size):
        chosen = jnp.where(by_old[k], every[:, : 2 * hidden_part], none)
        back += jnp.dot(
            chosen, weights_gu[k].reshape(2 * hidden_part, part), preferred_element_type=wide
        )
    back = back.astype(half)
    returned = jnp.stack(
        replica.exchange([back[k * rows : (k + 1) * rows] for k in range(replica.size)])
    )

    def block_of(device):
        start = device * column
        if column >= part:
            return jnp.concatenate(
                [
                    lax.dynamic_index_in_dim(
                        returned, replica.entry(start // part + j), axis=0, keepdims=False
                    )
                    for j in range(column // part)
                ],
                axis=1,
            )
        slab = lax.dynamic_index_in_dim(
            returned, replica.entry(start // part), axis=0, keepdims=False
        )
        return lax.dynamic_slice_in_dim(slab, start % part, column, axis=1)

    token_grad = shard.scatter_sum(
        [block_of(shard.peer(k)).astype(wide) for k in range(shard.size)]
    )

    owners = jnp.arange(owner.size, dtype=jnp.int32)
    holds = (new_place[:, None] == owners[None, :]).astype(jnp.int32)
    source_owner = jnp.sum(old_place[:, None] * holds, axis=0)

    def source_of(device):
        return jnp.sum(jnp.where(owners == device, source_owner, 0))

    moved_gu = pick(weights_gu, owner.entry(source_of(owner.me))).astype(wide)
    moved_d = pick(weights_d, owner.entry(source_of(owner.me))).astype(wide)
    moved_master = jnp.concatenate([moved_gu, moved_d[None]], axis=0)[None]
    moments = jnp.stack([moment_one[0].astype(half), moment_two[0].astype(half)])
    natural = hidden_part % owner.size == 0
    if natural:
        step = hidden_part // owner.size
        pieces = [moments[:, :, k * step : (k + 1) * step] for k in range(owner.size)]
    else:
        flat = moments.reshape(owner.size, -1)
        pieces = [flat[k] for k in range(owner.size)]
    parked = owner.exchange(pieces)
    sent = [
        pick(parked, owner.entry(source_of(owner.peer(k)))) for k in range(owner.size)
    ]
    landed = owner.exchange(sent)
    if owner.pairs:
        turn = owner.me ^ source_of(owner.me)
        landed = [pick(landed, turn ^ k) for k in range(owner.size)]
    if natural:
        moved = jnp.concatenate(landed, axis=2)
    else:
        moved = jnp.stack(landed).reshape(moments.shape)
    moved_one = moved[0].astype(wide)[None]
    moved_two = moved[1].astype(wide)[None]
    gradient = jnp.concatenate([gradient_gu, gradient_d[None]], axis=0)[None]
    master_out, first_out, second_out = adamw_step(moved_master, moved_one, moved_two, gradient)
    return (token_grad.astype(half), master_out, first_out, second_out)


def on_device_routed(
    tokens, out_grad, expert_ids, combine, old_place, new_place, master, moment_one, moment_two
):
    owner_count = lax.axis_size("expert")
    shard_count = lax.axis_size("shard")
    owners = jnp.arange(owner_count, dtype=jnp.int32)
    holds = (new_place[:, None] == owners[None, :]).astype(jnp.int32)
    source_owner = jnp.sum(old_place[:, None] * holds, axis=0)
    tok_rows, column = tokens.shape
    model_width = column * shard_count
    top_width = expert_ids.shape[1]
    assign = tok_rows * top_width
    capacity = 2 * tok_rows * top_width // owner_count
    slots_all = owner_count * capacity
    flat_ids = expert_ids.reshape(assign)
    onehot = (flat_ids[:, None] == owners[None, :]).astype(jnp.int32)
    earlier = jnp.cumsum(onehot, axis=0) - onehot
    slot = jnp.sum(earlier * onehot, axis=1)
    target = jnp.sum(onehot * new_place[None, :], axis=1)
    position = target * capacity + slot
    slot_ids = jnp.arange(slots_all, dtype=jnp.int32)
    match = position[None, :] == slot_ids[:, None]
    select = jnp.sum(match.reshape(slots_all, tok_rows, top_width).astype(jnp.float32), axis=2)
    slot_scale = jnp.sum(jnp.where(match, combine.reshape(1, assign), 0.0), axis=1)
    select_half = select.astype(jnp.bfloat16)
    rows_x = jnp.dot(select_half, tokens, preferred_element_type=jnp.float32).astype(jnp.bfloat16)
    rows_out = jnp.dot(select_half, out_grad, preferred_element_type=jnp.float32)
    rows_dy = (slot_scale[:, None] * rows_out).astype(jnp.bfloat16)
    arrived_x, arrived_dy = (
        lax.all_to_all(
            rows_x.reshape(owner_count, capacity, column),
            "expert",
            split_axis=0,
            concat_axis=0,
            tiled=True,
        ),
        lax.all_to_all(
            rows_dy.reshape(owner_count, capacity, column),
            "expert",
            split_axis=0,
            concat_axis=0,
            tiled=True,
        ),
    )
    whole_x, whole_dy = (
        lax.all_gather(arrived_x, "shard", axis=2, tiled=True),
        lax.all_gather(arrived_dy, "shard", axis=2, tiled=True),
    )
    piece_count = master.size // owner_count
    parked_master, parked_one, parked_two = (
        lax.all_to_all(
            master.reshape(owner_count, piece_count).astype(jnp.bfloat16),
            "expert",
            split_axis=0,
            concat_axis=0,
            tiled=True,
        ).astype(jnp.float32),
        lax.all_to_all(
            moment_one.reshape(owner_count, piece_count).astype(jnp.bfloat16),
            "expert",
            split_axis=0,
            concat_axis=0,
            tiled=True,
        ).astype(jnp.float32),
        lax.all_to_all(
            moment_two.reshape(owner_count, piece_count).astype(jnp.bfloat16),
            "expert",
            split_axis=0,
            concat_axis=0,
            tiled=True,
        ).astype(jnp.float32),
    )
    onward_master = jnp.take(parked_master, source_owner, axis=0)
    onward_one = jnp.take(parked_one, source_owner, axis=0)
    onward_two = jnp.take(parked_two, source_owner, axis=0)
    landed_master, landed_one, landed_two = (
        lax.all_to_all(
            onward_master.astype(jnp.bfloat16), "expert", split_axis=0, concat_axis=0, tiled=True
        ).astype(onward_master.dtype),
        lax.all_to_all(
            onward_one.astype(jnp.bfloat16), "expert", split_axis=0, concat_axis=0, tiled=True
        ).astype(onward_one.dtype),
        lax.all_to_all(
            onward_two.astype(jnp.bfloat16), "expert", split_axis=0, concat_axis=0, tiled=True
        ).astype(onward_two.dtype),
    )
    moved_master = landed_master.reshape(master.shape)
    moved_one = landed_one.reshape(master.shape)
    moved_two = landed_two.reshape(master.shape)
    full_weight = lax.all_gather(moved_master.astype(jnp.bfloat16), "dp", axis=3, tiled=True)[0]
    rows_in = whole_x.reshape(slots_all, model_width)
    rows_grad = whole_dy.reshape(slots_all, model_width)
    gate_up = jnp.einsum(
        "rd,gfd->grf", rows_in, full_weight[:2], preferred_element_type=jnp.float32
    )
    gate_pre = gate_up[0]
    up_pre = gate_up[1]
    sigma = jax.nn.sigmoid(gate_pre)
    active = gate_pre * sigma
    hidden = (active * up_pre).astype(jnp.bfloat16)
    grad_hidden = jnp.einsum(
        "rd,fd->rf", rows_grad, full_weight[2], preferred_element_type=jnp.float32
    )
    grad_up = (grad_hidden * active).astype(jnp.bfloat16)
    grad_gate = (grad_hidden * up_pre * sigma * (1.0 + gate_pre * (1.0 - sigma))).astype(
        jnp.bfloat16
    )
    partial_value = jnp.dot(
        grad_gate, full_weight[0], preferred_element_type=jnp.float32
    ) + jnp.dot(grad_up, full_weight[1], preferred_element_type=jnp.float32)
    weight_grad = jnp.stack(
        [
            jnp.einsum("rf,rd->fd", grad_gate, rows_in, preferred_element_type=jnp.float32),
            jnp.einsum("rf,rd->fd", grad_up, rows_in, preferred_element_type=jnp.float32),
            jnp.einsum("rf,rd->fd", hidden, rows_grad, preferred_element_type=jnp.float32),
        ],
        axis=0,
    )
    gradient = lax.psum_scatter(
        weight_grad.astype(jnp.bfloat16), "dp", scatter_dimension=2, tiled=True
    ).astype(jnp.float32)
    master_out, first_out, second_out = adamw_step(
        moved_master, moved_one, moved_two, gradient[None]
    )
    summed = lax.psum_scatter(
        partial_value.astype(jnp.bfloat16), "shard", scatter_dimension=1, tiled=True
    ).astype(jnp.float32)
    returned = lax.all_to_all(
        summed.reshape(owner_count, capacity, column).astype(jnp.bfloat16),
        "expert",
        split_axis=0,
        concat_axis=0,
        tiled=True,
    ).astype(jnp.float32)
    row_grad = returned.reshape(slots_all, column)
    token_grad = jnp.dot(select.T, row_grad, precision=lax.Precision.HIGHEST)
    return (token_grad.astype(jnp.bfloat16), master_out, first_out, second_out)


def solution(mesh):
    states = P("expert", None, "shard", "dp")
    in_specs = (
        P(("dp", "expert"), "shard"),
        P(("dp", "expert"), "shard"),
        P(("dp", "expert"), None),
        P(("dp", "expert"), None),
        P(),
        P(),
        states,
        states,
        states,
    )
    out_specs = (P(("dp", "expert"), "shard"), states, states, states)
    short = all(size in (1, 2, 4) for size in mesh.shape.values())
    return jax.shard_map(
        on_device if short else on_device_routed, mesh=mesh, in_specs=in_specs, out_specs=out_specs, check_vma=False
    )
```

```python
import jax
import jax.numpy as jnp
from jax import lax
from jax.sharding import PartitionSpec as P

beta_first = 0.9
beta_second = 0.95
adam_epsilon = 1e-08
learn_rate = 0.001
weight_decay = 0.1
bias_first = 1.0 - beta_first**10
bias_second = 1.0 - beta_second**10

half = jnp.bfloat16
wide = jnp.float32


def adamw_step(master, moment_one, moment_two, gradient):
    first_out = beta_first * moment_one + (1.0 - beta_first) * gradient
    second_out = beta_second * moment_two + (1.0 - beta_second) * gradient * gradient
    update = first_out / bias_first / (jnp.sqrt(second_out / bias_second) + adam_epsilon)
    master_out = master - learn_rate * (update + weight_decay * master)
    return (master_out, first_out, second_out)


class Axis:
    def __init__(self, name):
        self.name = name
        self.size = lax.axis_size(name)
        self.me = lax.axis_index(name)

    def swap(self, value, k):
        return lax.ppermute(value, self.name, [(i, i ^ k) for i in range(self.size)])

    def gather(self, value, relay):
        if self.size < 4:
            return [value] + [self.swap(value, k) for k in range(1, self.size)]
        one, two = self.swap(value, 1), self.swap(value, 2)
        return [value, one, two, self.swap(two if relay == 1 else one, relay)]

    def gather_pairs(self, value):
        if self.size < 4:
            return self.gather(value, 1)
        far = self.swap(value, 2)
        got = self.swap(jnp.concatenate([value, far], axis=0), 1)
        cut = value.shape[0]
        return [value, got[:cut], far, got[cut:]]

    def exchange(self, values):
        return [values[0]] + [self.swap(values[k], k) for k in range(1, self.size)]


def after(value, *deps):
    return lax.optimization_barrier((value, *deps))[0]


def pick(values, index):
    return lax.dynamic_index_in_dim(jnp.stack(values), index, axis=0, keepdims=False)


def rows_dot(a, b):
    return lax.dot_general(a, b, (((1,), (1,)), ((), ())), preferred_element_type=wide)


def sum_dot(a, b):
    return lax.dot_general(a, b, (((0,), (0,)), ((), ())), preferred_element_type=wide)


def on_device(
    tokens, out_grad, expert_ids, combine, old_place, new_place, master, moment_one, moment_two
):
    owner, shard, replica = Axis("expert"), Axis("shard"), Axis("dp")
    rows, column = tokens.shape
    part = master.shape[3]
    units = master.shape[2]
    per = column // part
    plane = rows * replica.size

    def block(value, k):
        return value[k * rows : (k + 1) * rows]

    weights = owner.gather(master[0].astype(half), relay=1)

    ids = jnp.concatenate(replica.gather_pairs(expert_ids.reshape(rows)), axis=0)
    named = ids[:, None] == jnp.arange(old_place.shape[0], dtype=jnp.int32)[None, :]
    old_owner = jnp.sum(jnp.where(named, old_place[None, :], 0), axis=1)[:, None]
    new_owner = jnp.sum(jnp.where(named, new_place[None, :], 0), axis=1)[:, None]

    def columns_of(value):
        every_column = shard.gather(value, 1)
        whole = jnp.stack(every_column)
        pieces = []
        for k in range(replica.size):
            device = replica.me ^ k
            slab = shard.me ^ lax.div(device, per)
            start = lax.rem(device, per) * part
            pieces.append(lax.dynamic_slice(whole, (slab, 0, start), (1, rows, part))[0])
        return pieces, every_column[-1]

    pieces_x, arrived_x = columns_of(tokens)
    scaled = (combine * out_grad.astype(wide)).astype(half)
    pieces_dy, _ = columns_of(after(scaled, arrived_x))
    rows_x = jnp.concatenate(replica.exchange(pieces_x), axis=0)
    rows_dy = jnp.concatenate(replica.exchange(pieces_dy), axis=0)

    none = jnp.zeros((), half)
    by_old = [old_owner == (owner.me ^ k) for k in range(owner.size)]
    by_new = [new_owner == (owner.me ^ k) for k in range(owner.size)]
    gate_up = jnp.zeros((plane, 2 * units), wide)
    grad_hid = jnp.zeros((plane, units), wide)
    for k in range(owner.size):
        gate_up += rows_dot(
            jnp.where(by_old[k], rows_x, none), weights[k][:2].reshape(2 * units, part)
        )
        grad_hid += rows_dot(jnp.where(by_old[k], rows_dy, none), weights[k][2])
    products = jnp.concatenate([gate_up, grad_hid], axis=1)
    own = block(products, 0)
    if replica.size == 4:
        near = replica.swap(
            jnp.stack([block(products, 1), block(products, 3)]).astype(half), 1
        )
        own = own + near[0].astype(wide)
        far = block(products, 2) + near[1].astype(wide)
        own = own + replica.swap(far.astype(half), 2).astype(wide)
    else:
        for k in range(1, replica.size):
            own = own + replica.swap(block(products, k).astype(half), k).astype(wide)
    gate_pre = own[:, :units]
    up_pre = own[:, units : 2 * units]
    grad_hidden = own[:, 2 * units :]
    sigma = jax.nn.sigmoid(gate_pre)
    active = gate_pre * sigma
    hidden = (active * up_pre).astype(half)
    grad_up = (grad_hidden * active).astype(half)
    grad_gate = (grad_hidden * up_pre * sigma * (1.0 + gate_pre * (1.0 - sigma))).astype(half)
    local = jnp.concatenate([grad_gate, grad_up, hidden], axis=1)
    every = jnp.concatenate(replica.gather_pairs(local), axis=0)

    owners = jnp.arange(owner.size, dtype=jnp.int32)
    holds = (new_place[:, None] == owners[None, :]).astype(jnp.int32)
    source_owner = jnp.sum(old_place[:, None] * holds, axis=0)

    def source_of(device):
        return jnp.sum(jnp.where(owners == device, source_owner, 0))

    moments = jnp.stack([moment_one[0].astype(half), moment_two[0].astype(half)])
    step = units // owner.size
    pieces = [
        after(moments[:, :, k * step : (k + 1) * step], weights[min(2, owner.size - 1)])
        for k in range(owner.size)
    ]
    parked = owner.exchange(pieces)
    parked = [after(p, local) for p in parked]
    sent = [
        pick(parked, owner.me ^ source_of(owner.me ^ k)) for k in range(owner.size)
    ]
    landed = owner.exchange(sent)

    def grads_of(k):
        chosen = jnp.where(by_new[k], every, none)
        return jnp.concatenate(
            [
                sum_dot(chosen[:, : 2 * units], rows_x).reshape(2, units, part),
                sum_dot(chosen[:, 2 * units :], rows_dy)[None],
            ],
            axis=0,
        )

    grads = [grads_of(k) for k in range(owner.size)]
    gradient = grads[0]
    if owner.size == 4:
        near = owner.swap(grads[3].astype(half), 1).astype(wide)
        side = owner.swap(grads[1].astype(half), 1).astype(wide)
        far = owner.swap((grads[2] + near).astype(half), 2).astype(wide)
        gradient = gradient + side + far
    else:
        for k in range(1, owner.size):
            gradient = gradient + owner.swap(grads[k].astype(half), k).astype(wide)

    back = jnp.zeros((plane, part), wide)
    for k in range(owner.size):
        chosen = jnp.where(by_old[k], every[:, : 2 * units], none)
        back += jnp.dot(
            chosen, weights[k][:2].reshape(2 * units, part), preferred_element_type=wide
        )
    back = back.astype(half)
    returned = jnp.stack(replica.exchange([block(back, k) for k in range(replica.size)]))

    def block_of(device):
        return jnp.concatenate(
            [
                lax.dynamic_index_in_dim(
                    returned, replica.me ^ (device * per + j), axis=0, keepdims=False
                )
                for j in range(per)
            ],
            axis=1,
        )

    token_grad = block_of(shard.me).astype(wide)
    for k in range(1, shard.size):
        token_grad = token_grad + shard.swap(block_of(shard.me ^ k), k).astype(wide)

    source = owner.me ^ source_of(owner.me)
    moved_master = pick(weights, source).astype(wide)
    moved = jnp.concatenate([pick(landed, source ^ k) for k in range(owner.size)], axis=2)
    master_out, first_out, second_out = adamw_step(
        moved_master, moved[0].astype(wide), moved[1].astype(wide), gradient
    )
    return (token_grad.astype(half), master_out[None], first_out[None], second_out[None])


def on_device_routed(
    tokens, out_grad, expert_ids, combine, old_place, new_place, master, moment_one, moment_two
):
    owner_count = lax.axis_size("expert")
    shard_count = lax.axis_size("shard")
    owners = jnp.arange(owner_count, dtype=jnp.int32)
    holds = (new_place[:, None] == owners[None, :]).astype(jnp.int32)
    source_owner = jnp.sum(old_place[:, None] * holds, axis=0)
    tok_rows, column = tokens.shape
    model_width = column * shard_count
    top_width = expert_ids.shape[1]
    assign = tok_rows * top_width
    capacity = 2 * tok_rows * top_width // owner_count
    slots_all = owner_count * capacity
    flat_ids = expert_ids.reshape(assign)
    onehot = (flat_ids[:, None] == owners[None, :]).astype(jnp.int32)
    earlier = jnp.cumsum(onehot, axis=0) - onehot
    slot = jnp.sum(earlier * onehot, axis=1)
    target = jnp.sum(onehot * new_place[None, :], axis=1)
    position = target * capacity + slot
    slot_ids = jnp.arange(slots_all, dtype=jnp.int32)
    match = position[None, :] == slot_ids[:, None]
    select = jnp.sum(match.reshape(slots_all, tok_rows, top_width).astype(jnp.float32), axis=2)
    slot_scale = jnp.sum(jnp.where(match, combine.reshape(1, assign), 0.0), axis=1)
    select_half = select.astype(jnp.bfloat16)
    rows_x = jnp.dot(select_half, tokens, preferred_element_type=jnp.float32).astype(jnp.bfloat16)
    rows_out = jnp.dot(select_half, out_grad, preferred_element_type=jnp.float32)
    rows_dy = (slot_scale[:, None] * rows_out).astype(jnp.bfloat16)
    arrived_x, arrived_dy = (
        lax.all_to_all(
            rows_x.reshape(owner_count, capacity, column),
            "expert",
            split_axis=0,
            concat_axis=0,
            tiled=True,
        ),
        lax.all_to_all(
            rows_dy.reshape(owner_count, capacity, column),
            "expert",
            split_axis=0,
            concat_axis=0,
            tiled=True,
        ),
    )
    whole_x, whole_dy = (
        lax.all_gather(arrived_x, "shard", axis=2, tiled=True),
        lax.all_gather(arrived_dy, "shard", axis=2, tiled=True),
    )
    piece_count = master.size // owner_count
    parked_master, parked_one, parked_two = (
        lax.all_to_all(
            master.reshape(owner_count, piece_count).astype(jnp.bfloat16),
            "expert",
            split_axis=0,
            concat_axis=0,
            tiled=True,
        ).astype(jnp.float32),
        lax.all_to_all(
            moment_one.reshape(owner_count, piece_count).astype(jnp.bfloat16),
            "expert",
            split_axis=0,
            concat_axis=0,
            tiled=True,
        ).astype(jnp.float32),
        lax.all_to_all(
            moment_two.reshape(owner_count, piece_count).astype(jnp.bfloat16),
            "expert",
            split_axis=0,
            concat_axis=0,
            tiled=True,
        ).astype(jnp.float32),
    )
    onward_master = jnp.take(parked_master, source_owner, axis=0)
    onward_one = jnp.take(parked_one, source_owner, axis=0)
    onward_two = jnp.take(parked_two, source_owner, axis=0)
    landed_master, landed_one, landed_two = (
        lax.all_to_all(
            onward_master.astype(jnp.bfloat16), "expert", split_axis=0, concat_axis=0, tiled=True
        ).astype(onward_master.dtype),
        lax.all_to_all(
            onward_one.astype(jnp.bfloat16), "expert", split_axis=0, concat_axis=0, tiled=True
        ).astype(onward_one.dtype),
        lax.all_to_all(
            onward_two.astype(jnp.bfloat16), "expert", split_axis=0, concat_axis=0, tiled=True
        ).astype(onward_two.dtype),
    )
    moved_master = landed_master.reshape(master.shape)
    moved_one = landed_one.reshape(master.shape)
    moved_two = landed_two.reshape(master.shape)
    full_weight = lax.all_gather(moved_master.astype(jnp.bfloat16), "dp", axis=3, tiled=True)[0]
    rows_in = whole_x.reshape(slots_all, model_width)
    rows_grad = whole_dy.reshape(slots_all, model_width)
    gate_up = jnp.einsum(
        "rd,gfd->grf", rows_in, full_weight[:2], preferred_element_type=jnp.float32
    )
    gate_pre = gate_up[0]
    up_pre = gate_up[1]
    sigma = jax.nn.sigmoid(gate_pre)
    active = gate_pre * sigma
    hidden = (active * up_pre).astype(jnp.bfloat16)
    grad_hidden = jnp.einsum(
        "rd,fd->rf", rows_grad, full_weight[2], preferred_element_type=jnp.float32
    )
    grad_up = (grad_hidden * active).astype(jnp.bfloat16)
    grad_gate = (grad_hidden * up_pre * sigma * (1.0 + gate_pre * (1.0 - sigma))).astype(
        jnp.bfloat16
    )
    partial_value = jnp.dot(
        grad_gate, full_weight[0], preferred_element_type=jnp.float32
    ) + jnp.dot(grad_up, full_weight[1], preferred_element_type=jnp.float32)
    weight_grad = jnp.stack(
        [
            jnp.einsum("rf,rd->fd", grad_gate, rows_in, preferred_element_type=jnp.float32),
            jnp.einsum("rf,rd->fd", grad_up, rows_in, preferred_element_type=jnp.float32),
            jnp.einsum("rf,rd->fd", hidden, rows_grad, preferred_element_type=jnp.float32),
        ],
        axis=0,
    )
    gradient = lax.psum_scatter(
        weight_grad.astype(jnp.bfloat16), "dp", scatter_dimension=2, tiled=True
    ).astype(jnp.float32)
    master_out, first_out, second_out = adamw_step(
        moved_master, moved_one, moved_two, gradient[None]
    )
    summed = lax.psum_scatter(
        partial_value.astype(jnp.bfloat16), "shard", scatter_dimension=1, tiled=True
    ).astype(jnp.float32)
    returned = lax.all_to_all(
        summed.reshape(owner_count, capacity, column).astype(jnp.bfloat16),
        "expert",
        split_axis=0,
        concat_axis=0,
        tiled=True,
    ).astype(jnp.float32)
    row_grad = returned.reshape(slots_all, column)
    token_grad = jnp.dot(select.T, row_grad, precision=lax.Precision.HIGHEST)
    return (token_grad.astype(jnp.bfloat16), master_out, first_out, second_out)


def solution(mesh):
    states = P("expert", None, "shard", "dp")
    in_specs = (
        P(("dp", "expert"), "shard"),
        P(("dp", "expert"), "shard"),
        P(("dp", "expert"), None),
        P(("dp", "expert"), None),
        P(),
        P(),
        states,
        states,
        states,
    )
    out_specs = (P(("dp", "expert"), "shard"), states, states, states)
    short = all(size in (1, 2, 4) for size in mesh.shape.values())
    return jax.shard_map(
        on_device if short and mesh.shape["dp"] % mesh.shape["shard"] == 0 else on_device_routed,
        mesh=mesh,
        in_specs=in_specs,
        out_specs=out_specs,
        check_vma=False,
    )
```
